32 devices in a mesh: heads: 4 (over y, core), seq: 8 (over z, x).
Axes of the slice: x: 2, y: 2, z: 4, core: 2. Of those that a mesh axis runs over, the one named last changes fastest.
Arguments:
- queries: bfloat16 [1024, 64, 576], P('seq', 'heads'), may hold values from -6 to 6
- latents: bfloat16 [8, 128, 576], P('seq', 'heads'), may hold values from -6 to 6
- grad_out: bfloat16 [1024, 64, 512], P('seq', 'heads'), may hold values from -6 to 6
- selected: int32 [8, 4], P('seq'), may hold values from 0 to 7, as said below
Outputs:
- output: bfloat16 [1024, 64, 512], P('seq', 'heads')
- grad_query: bfloat16 [1024, 64, 576], P('seq', 'heads')
- latent_grad: float32 [8, 128, 576], P('seq', 'heads')
The draws below stay inside these ranges and needn't reach their ends.
Inputs may be any that keep to these rules, and one draw needn't show every extreme that they name: `selected`: row i lists 4 different blocks, none of them held on the same index of seq as block i (blocks i and j share it when i // 1 equals j // 1); how often a block is chosen varies widely between blocks.
All inputs are finite; a program needn't handle non-finite values.
Results may differ from the reference program's by a relative error of at most 0.012.
Values may be sent and summed in bfloat16 or wider, within the bound.
A program may use at most 64 MiB of HBM per device.

```python
import jax
import jax.numpy as jnp
from jax import lax

HEADS = 64
LATENT = 512
BLOCK = 128
TOP = 4
DK = 576
QUERY_BLOCK_UNIT = 1
SEQ = 1024
NBLK = 8


def draw_latents(key, part):
    values = jnp.clip(jax.random.normal(jax.random.fold_in(key, 11), (NBLK, BLOCK, DK), jnp.float32), -6.0, 6.0)
    return values.astype(jnp.bfloat16)


def draw_queries(key, part):
    values = jnp.clip(jax.random.normal(jax.random.fold_in(key, 12), (SEQ, HEADS, DK), jnp.float32), -6.0, 6.0)
    return values.astype(jnp.bfloat16)


def draw_selected(key, part):
    popular = jax.random.randint(jax.random.fold_in(key, 21), (NBLK,), 0, 5)
    weight = (popular + 1) * (popular + 1)
    noise = jax.random.randint(jax.random.fold_in(key, 22), (NBLK, NBLK), 0, 4096)
    column_span = jnp.arange(NBLK, dtype=jnp.int32)
    scores = noise * weight[None, :] * NBLK + column_span[None, :]
    holder = column_span // QUERY_BLOCK_UNIT
    scores = jnp.where(holder[:, None] == holder[None, :], -1, scores)
    _, chosen = lax.top_k(scores, TOP)
    return chosen.astype(jnp.int32)


def levels(key, shape, split, smallest, top_value):
    loudness, own = 1.0, jax.random.fold_in(key, 6)
    for axis_at, shards_of in split:
        steps = jnp.exp(jax.random.uniform(jax.random.fold_in(own, axis_at), (shards_of,), jnp.float32, smallest / len(split), top_value / len(split)))
        loudness = loudness * jnp.repeat(steps, shape[axis_at] // shards_of).reshape([-1 if axis == axis_at else 1 for axis in range(len(shape))])
    return loudness


def scatter_about(key, shape, spread, bound, shards=(), kind=jnp.bfloat16):
    array = spread * jax.random.normal(key, shape, jnp.float32)
    if shards:
        array = array * levels(key, shape, shards, -0.22, 0.18)
    return jnp.clip(array, -bound, bound).astype(kind)


def setup_inputs(seed: int = 0) -> dict:
    arg_keys = jax.random.split(jax.random.key(seed), 5)
    return {
        "queries": draw_queries(jax.random.fold_in(arg_keys[4], 71), 0),
        "latents": draw_latents(jax.random.fold_in(arg_keys[4], 71), 0),
        "grad_out": scatter_about(arg_keys[2], (SEQ, HEADS, LATENT), 1.0, 6.0, ((0, 8), (1, 4))),
        "selected": draw_selected(jax.random.fold_in(arg_keys[4], 71), 0),
    }


def reference(queries, latents, grad_out, selected):
    list_blocks, block_size, key_width = latents.shape
    token_total, head_count, _ = queries.shape
    value_width = grad_out.shape[2]
    score_scale = key_width ** -0.5
    query_blocks = queries.reshape(list_blocks, block_size, head_count, key_width)
    grad_blocks = grad_out.reshape(list_blocks, block_size, head_count, value_width)
    own_blocks = jnp.arange(list_blocks, dtype=jnp.int32)[:, None]
    block_ids = jnp.concatenate([own_blocks, selected.astype(jnp.int32)], axis=1)

    def block_step(totals, pieces):
        query_row_tiles, grad_rows, key_ids = pieces
        key_row_tiles = latents[key_ids].reshape(-1, key_width).astype(jnp.float32)
        query_full = query_row_tiles.astype(jnp.float32)
        grad_full = grad_rows.astype(jnp.float32)
        value_rows = key_row_tiles[:, :value_width]
        scores = jnp.einsum('thd,kd->htk', query_full, key_row_tiles) * score_scale
        prob_full = jax.nn.softmax(scores, axis=-1)
        prob_half = prob_full.astype(jnp.bfloat16)
        output = jnp.einsum('htk,kl->thl', prob_half.astype(jnp.float32), value_rows).astype(jnp.bfloat16)
        row_delta = jnp.sum(grad_full * output.astype(jnp.float32), axis=-1)
        grad_prob = jnp.einsum('thl,kl->htk', grad_full, value_rows)
        score_gradient = (prob_full * (grad_prob - row_delta.T[:, :, None]) * score_scale).astype(jnp.bfloat16)
        grad_query = jnp.einsum('htk,kd->thd', score_gradient.astype(jnp.float32), key_row_tiles).astype(jnp.bfloat16)
        key_gradient = jnp.einsum('htk,thd->kd', score_gradient.astype(jnp.float32), query_full)
        grad_value = jnp.einsum('htk,thl->kl', prob_half.astype(jnp.float32), grad_full)
        key_gradient = key_gradient.at[:, :value_width].add(grad_value)
        totals = totals.at[key_ids].add(key_gradient.reshape(-1, block_size, key_width))
        return totals, (output, grad_query)

    start_grad = jnp.zeros((list_blocks, block_size, key_width), jnp.float32)
    latent_grad, (output, grad_query) = lax.scan(block_step, start_grad, (query_blocks, grad_blocks, block_ids))
    return (output.reshape(token_total, head_count, value_width),
            grad_query.reshape(token_total, head_count, key_width),
            latent_grad)
```

```python
import functools

import jax
import jax.numpy as jnp
from jax import lax
from jax.experimental import pallas as pl
from jax.experimental.pallas import tpu as pltpu
from jax.sharding import PartitionSpec as P

MESH = pl.DeviceIdType.MESH
VMEM = pltpu.MemorySpace.VMEM
SMEM = pltpu.MemorySpace.SMEM


def place(dims):
    a_n, b_n, g_n, c_n = dims
    s, h = lax.axis_index("seq"), lax.axis_index("heads")
    return s // b_n, lax.rem(s, b_n), h // c_n, lax.rem(h, c_n)


def other(x, k, n):
    return lax.rem(x + k, n)


def greet(dims, me):
    a_n, b_n, g_n, c_n = dims
    a, b, g, c = me
    barrier = pltpu.get_barrier_semaphore()

    def signal(a2, b2, g2, c2):
        pl.semaphore_signal(
            barrier, inc=1, device_id=(g2 * c_n + c2, a2 * b_n + b2), device_id_type=MESH
        )

    for k in range(1, c_n):
        signal(a, b, g, other(c, k, c_n))
    for k in range(1, b_n):
        signal(a, other(b, k, b_n), g, c)
    for k in range(1, g_n):
        signal(a, b, other(g, k, g_n), c)
    for k in range(1, a_n):
        signal(other(a, k, a_n), b, g, c)
    pl.semaphore_wait(barrier, a_n + b_n + g_n + c_n - 4)


def gather_kernel(dims, own_ref, out_ref, own_sem, a_sem, b_sem, g_sem, c_sem, recv_sem):
    a_n, b_n, g_n, c_n = dims
    me = place(dims)
    a, b, g, c = me
    mine = pltpu.make_async_copy(own_ref.at[0], out_ref.at[a * b_n + b, g * c_n + c], own_sem)
    mine.start()
    greet(dims, me)

    def copy(piece, target, sem, own=False):
        a1, b1, g1, c1 = piece
        a2, b2, g2, c2 = target
        slot = (a1 * b_n + b1, g1 * c_n + c1)
        return pltpu.make_async_remote_copy(
            src_ref=own_ref.at[0] if own else out_ref.at[slot],
            dst_ref=out_ref.at[slot],
            send_sem=sem,
            recv_sem=recv_sem.at[slot],
            device_id=(g2 * c_n + c2, a2 * b_n + b2),
            device_id_type=MESH,
        )

    def to_a(k, own=True):
        return copy(me, (other(a, k, a_n), b, g, c), a_sem.at[k], own)

    def to_b(piece, k, own=False):
        return copy(piece, (a, other(b, k, b_n), g, c), b_sem.at[piece[0], k], own)

    def to_g(piece, k, own=False):
        return copy(
            piece, (a, b, other(g, k, g_n), c), g_sem.at[piece[0] * b_n + piece[1], k], own
        )

    def to_c(piece, k, own=False):
        return copy(
            piece,
            (a, b, g, other(c, k, c_n)),
            c_sem.at[piece[0] * b_n + piece[1], piece[2], k],
            own,
        )

    def arrived(piece):
        copy(piece, (a, b, g, c), own_sem).wait_recv()

    for k in range(1, a_n):
        to_a(k).start()
    for k in range(1, g_n):
        to_g(me, k, True).start()
    for k in range(1, b_n):
        to_b(me, k, True).start()
    for k in range(1, c_n):
        to_c(me, k, True).start()

    def forward(k, first):
        a1 = other(a, k, a_n)
        piece = (a1, b, g, c)
        if not first:
            arrived(piece)
            for n in range(1, g_n):
                to_g(piece, n).start()
            for n in range(1, b_n):
                to_b(piece, n).start()
            for n in range(1, c_n):
                to_c(piece, n).start()
        for n in range(1, b_n):
            piece = (a1, other(b, n, b_n), g, c)
            arrived(piece)
            for m in range(1, g_n):
                to_g(piece, m).start()
            for m in range(1, c_n):
                to_c(piece, m).start()
        for n in range(b_n):
            for m in range(1, g_n):
                piece = (a1, other(b, n, b_n), other(g, m, g_n), c)
                arrived(piece)
                for i in range(1, c_n):
                    to_c(piece, i).start()

    forward(0, True)
    if a_n > 1:
        lax.fori_loop(1, a_n, lambda k, _: (forward(k, False), 0)[1], 0)

    def finish(k, _):
        a1 = other(a, k, a_n)
        for n in range(b_n):
            b1 = other(b, n, b_n)
            for m in range(1, g_n):
                to_g((a1, b1, g, c), m).wait_send()
            for m in range(g_n):
                g1 = other(g, m, g_n)
                for i in range(1, c_n):
                    to_c((a1, b1, g1, c), i).wait_send()
                    arrived((a1, b1, g1, other(c, i, c_n)))
        for n in range(1, b_n):
            to_b((a1, b, g, c), n).wait_send()
        return 0

    lax.fori_loop(0, a_n, finish, 0)
    for k in range(1, a_n):
        to_a(k).wait_send()
    mine.wait()


def gather_latents(latents, dims):
    a_n, b_n, g_n, c_n = dims
    _, row_share, key_width = latents.shape
    n_s, n_h = a_n * b_n, g_n * c_n
    dma = pltpu.SemaphoreType.DMA
    return pl.pallas_call(
        functools.partial(gather_kernel, dims),
        out_shape=jax.ShapeDtypeStruct((n_s, n_h, row_share, key_width), latents.dtype),
        in_specs=[pl.BlockSpec(memory_space=VMEM)],
        out_specs=pl.BlockSpec(memory_space=VMEM),
        scratch_shapes=[
            dma,
            dma((a_n,)),
            dma((a_n, b_n)),
            dma((n_s, g_n)),
            dma((n_s, g_n, c_n)),
            dma((n_s, n_h)),
        ],
        compiler_params=pltpu.CompilerParams(collective_id=0, has_side_effects=True),
        name="gather_latents",
    )(latents)


def attend_kernel(
    scale, value_width, sel_ref, all_ref, q_ref, g_ref, o_ref, dq_ref, con_ref, keys, acc
):
    step = pl.program_id(0)
    block = all_ref.shape[1]
    count = sel_ref.shape[1] + 1

    @pl.when(step == 0)
    def _():
        keys[:block, :] = all_ref[lax.axis_index("seq")]
        for n in range(1, count):
            keys[n * block : (n + 1) * block, :] = all_ref[sel_ref[0, n - 1]]
        acc[...] = jnp.zeros_like(acc)

    f32 = jnp.float32
    q, g = q_ref[...], g_ref[...]
    across = (((1,), (1,)), ((), ()))
    down = (((0,), (0,)), ((), ()))
    scores = lax.dot_general(q, keys[...], across, preferred_element_type=f32)
    top = jnp.max(scores, axis=-1, keepdims=True)
    weights = jnp.exp((scores - top) * scale)
    probs = weights * (1.0 / jnp.sum(weights, axis=-1, keepdims=True))
    half = probs.astype(jnp.bfloat16)
    values = keys[:, :value_width]
    out = jnp.dot(half, values, preferred_element_type=f32).astype(jnp.bfloat16)
    o_ref[...] = out
    delta = jnp.sum(g.astype(f32) * out.astype(f32), axis=-1, keepdims=True)
    grad_prob = lax.dot_general(g, values, across, preferred_element_type=f32)
    grad_score = (probs * (grad_prob - delta) * scale).astype(jnp.bfloat16)
    dq_ref[...] = jnp.dot(grad_score, keys[...], preferred_element_type=f32).astype(jnp.bfloat16)
    acc[...] += lax.dot_general(grad_score, q, down, preferred_element_type=f32)
    acc[:, :value_width] += lax.dot_general(half, g, down, preferred_element_type=f32)

    @pl.when(step == pl.num_programs(0) - 1)
    def _():
        con_ref[...] = acc[...].astype(jnp.bfloat16)


def attend(selected, all_keys, queries, grad_out):
    rows, key_width = queries.shape
    value_width = grad_out.shape[1]
    keys = (selected.shape[1] + 1) * all_keys.shape[1]
    tile = min(rows, 256)
    return pl.pallas_call(
        functools.partial(attend_kernel, key_width ** (-0.5), value_width),
        grid=(rows // tile,),
        out_shape=(
            jax.ShapeDtypeStruct((rows, value_width), jnp.bfloat16),
            jax.ShapeDtypeStruct((rows, key_width), jnp.bfloat16),
            jax.ShapeDtypeStruct((keys, key_width), jnp.bfloat16),
        ),
        in_specs=[
            pl.BlockSpec(memory_space=SMEM),
            pl.BlockSpec(all_keys.shape, lambda i: (0, 0, 0)),
            pl.BlockSpec((tile, key_width), lambda i: (i, 0)),
            pl.BlockSpec((tile, value_width), lambda i: (i, 0)),
        ],
        out_specs=(
            pl.BlockSpec((tile, value_width), lambda i: (i, 0)),
            pl.BlockSpec((tile, key_width), lambda i: (i, 0)),
            pl.BlockSpec((keys, key_width), lambda i: (0, 0)),
        ),
        scratch_shapes=[
            pltpu.VMEM((keys, key_width), jnp.bfloat16),
            pltpu.VMEM((keys, key_width), jnp.float32),
        ],
        name="attend",
    )(selected, all_keys, queries, grad_out)


def reduce_kernel(
    dims, sel_ref, con_ref, out_ref,
    c_in, g_out, g_in, sums, b_out, b_in, a_out, a_in,
    c_sem, g_sem, b_sem, a_sem,
):
    a_n, b_n, g_n, c_n = dims
    me = place(dims)
    a, b, g, c = me
    count = con_ref.shape[0]
    f32, bf16 = jnp.float32, jnp.bfloat16
    greet(dims, me)

    def copy(src, dst, sems, there):
        a2, b2, g2, c2 = there
        return pltpu.make_async_remote_copy(
            src_ref=src,
            dst_ref=dst,
            send_sem=sems.at[0],
            recv_sem=sems.at[1],
            device_id=(g2 * c_n + c2, a2 * b_n + b2),
            device_id_type=MESH,
        )

    def to_c(p, k):
        c2 = other(c, k, c_n)
        return copy(con_ref.at[p, :, c2], c_in.at[p, k], c_sem.at[p, k], (a, b, g, c2))

    def to_g(p, k):
        return copy(g_out.at[p, k], g_in.at[p, k], g_sem.at[p, k], (a, b, other(g, k, g_n), c))

    def to_b(k, n):
        return copy(b_out.at[k, n], b_in.at[k, n], b_sem.at[k, n], (a, other(b, n, b_n), g, c))

    def to_a(k):
        return copy(a_out.at[k], a_in.at[k], a_sem.at[k], (other(a, k, a_n), b, g, c))

    for p in range(count):
        for k in range(1, c_n):
            to_c(p, k).start()

    def chip_sum(p, g1):
        total = con_ref[p, g1, c].astype(f32)
        for k in range(1, c_n):
            total += c_in[p, k, g1].astype(f32)
        return total

    for p in range(count):
        for k in range(1, c_n):
            to_c(p, k).wait_recv()
        for k in range(1, g_n):
            g_out[p, k] = chip_sum(p, other(g, k, g_n)).astype(bf16)
            to_g(p, k).start()
    sums[count] = jnp.zeros(sums.shape[1:], f32)
    for p in range(count):
        total = chip_sum(p, g)
        for k in range(1, g_n):
            to_g(p, k).wait_recv()
            total += g_in[p, k].astype(f32)
        sums[p] = total

    def dense(a1, b1):
        block = a1 * b_n + b1
        at = jnp.where(block == a * b_n + b, 0, count)
        for n in range(1, count):
            at = jnp.where(sel_ref[0, n - 1] == block, n, at)
        return sums[at]

    def send_b(k, _):
        for n in range(1, b_n):
            b_out[k, n] = dense(other(a, k, a_n), other(b, n, b_n)).astype(bf16)
            to_b(k, n).start()
        return 0

    def send_a(k, _):
        total = dense(other(a, k, a_n), b)
        for n in range(1, b_n):
            to_b(k, n).wait_recv()
            total += b_in[k, n].astype(f32)
        a_out[k] = total.astype(bf16)
        to_a(k).start()
        return 0

    if b_n > 1:
        lax.fori_loop(1, a_n, send_b, 0)
        send_b(0, 0)
    lax.fori_loop(1, a_n, send_a, 0)
    total = dense(a, b)
    for n in range(1, b_n):
        to_b(0, n).wait_recv()
        total += b_in[0, n].astype(f32)
    out_ref[...] = total

    def take_a(k, _):
        to_a(k).wait_recv()
        out_ref[...] += a_in[k].astype(f32)
        return 0

    lax.fori_loop(1, a_n, take_a, 0)

    def finish(k, _):
        to_a(k).wait_send()
        for n in range(1, b_n):
            to_b(k, n).wait_send()
        return 0

    lax.fori_loop(1, a_n, finish, 0)
    for n in range(1, b_n):
        to_b(0, n).wait_send()
    for p in range(count):
        for k in range(1, c_n):
            to_c(p, k).wait_send()
        for k in range(1, g_n):
            to_g(p, k).wait_send()


def reduce_grads(selected, contrib, dims):
    a_n, b_n, g_n, c_n = dims
    count = selected.shape[1] + 1
    keys, key_width = contrib.shape
    rows = keys // count // (g_n * c_n)
    contrib = contrib.reshape(count, g_n, c_n, rows, key_width)
    one = (rows, key_width)
    dma = pltpu.SemaphoreType.DMA
    half = functools.partial(pltpu.VMEM, dtype=jnp.bfloat16)
    return pl.pallas_call(
        functools.partial(reduce_kernel, dims),
        out_shape=jax.ShapeDtypeStruct(one, jnp.float32),
        in_specs=[pl.BlockSpec(memory_space=SMEM), pl.BlockSpec(memory_space=VMEM)],
        out_specs=pl.BlockSpec(memory_space=VMEM),
        scratch_shapes=[
            half((count, c_n, g_n) + one),
            half((count, g_n) + one),
            half((count, g_n) + one),
            pltpu.VMEM((count + 1,) + one, jnp.float32),
            half((a_n, b_n) + one),
            half((a_n, b_n) + one),
            half((a_n,) + one),
            half((a_n,) + one),
            dma((count, c_n, 2)),
            dma((count, g_n, 2)),
            dma((a_n, b_n, 2)),
            dma((a_n, 2)),
        ],
        compiler_params=pltpu.CompilerParams(collective_id=1, has_side_effects=True),
        name="reduce_grads",
    )(selected, contrib)


def shards(dims, queries, latents, grad_out, selected):
    block_count, row_share, key_width = latents.shape
    token_total, head_count, _ = queries.shape
    value_width = grad_out.shape[2]
    assert block_count == 1
    rows = token_total * head_count
    pieces = gather_latents(latents, dims)
    all_keys = pieces.reshape(pieces.shape[0], -1, key_width)
    output, grad_query, contrib = attend(
        selected, all_keys, queries.reshape(rows, key_width), grad_out.reshape(rows, value_width)
    )
    latent_grad = reduce_grads(selected, contrib, dims)
    return (
        output.reshape(token_total, head_count, value_width),
        grad_query.reshape(token_total, head_count, key_width),
        latent_grad[None],
    )


def solution(mesh):
    n_h, n_s = mesh.shape["heads"], mesh.shape["seq"]
    b_n = 2 if n_s % 2 == 0 else 1
    c_n = 2 if n_h % 2 == 0 else 1
    dims = (n_s // b_n, b_n, n_h // c_n, c_n)
    in_specs = (
        P("seq", "heads", None),
        P("seq", "heads", None),
        P("seq", "heads", None),
        P("seq", None),
    )
    out_specs = (P("seq", "heads", None), P("seq", "heads", None), P("seq", "heads", None))
    return jax.shard_map(
        functools.partial(shards, dims),
        mesh=mesh, in_specs=in_specs, out_specs=out_specs, check_vma=False,
    )
```

```python
import functools

import jax
import jax.numpy as jnp
from jax import lax
from jax.experimental import pallas as pl
from jax.experimental.pallas import tpu as pltpu
from jax.sharding import PartitionSpec as P

MESH = pl.DeviceIdType.MESH
VMEM = pltpu.MemorySpace.VMEM
SMEM = pltpu.MemorySpace.SMEM


def place(dims):
    a_n, b_n, g_n, c_n = dims
    s, h = lax.axis_index("seq"), lax.axis_index("heads")
    return s // b_n, lax.rem(s, b_n), h // c_n, lax.rem(h, c_n)


def other(x, k, n):
    return lax.rem(x + k, n)


def greet(dims, me):
    a_n, b_n, g_n, c_n = dims
    a, b, g, c = me
    barrier = pltpu.get_barrier_semaphore()

    def signal(a2, b2, g2, c2):
        pl.semaphore_signal(
            barrier, inc=1, device_id=(g2 * c_n + c2, a2 * b_n + b2), device_id_type=MESH
        )

    for k in range(1, c_n):
        signal(a, b, g, other(c, k, c_n))
    for k in range(1, b_n):
        signal(a, other(b, k, b_n), g, c)
    for k in range(1, g_n):
        signal(a, b, other(g, k, g_n), c)
    for k in range(1, a_n):
        signal(other(a, k, a_n), b, g, c)
    pl.semaphore_wait(barrier, a_n + b_n + g_n + c_n - 4)


def gather_kernel(dims, own_ref, out_ref, own_sem, a_sem, b_sem, g_sem, c_sem, recv_sem):
    a_n, b_n, g_n, c_n = dims
    me = place(dims)
    a, b, g, c = me
    mine = pltpu.make_async_copy(own_ref.at[0], out_ref.at[a * b_n + b, g * c_n + c], own_sem)
    mine.start()
    greet(dims, me)

    swap = b_n == g_n
    flip = lax.rem(c, 2) if swap else 0

    def spot(ka, kp, kq, kc):
        kb, kg = (flip * kp + (1 - flip) * kq, (1 - flip) * kp + flip * kq) if swap else (kq, kp)
        return other(a, ka, a_n), other(b, kb, b_n), other(g, kg, g_n), other(c, kc, c_n)

    p_n, q_n = g_n, b_n

    def copy(key, step, sem, own):
        a1, b1, g1, c1 = spot(*key)
        a2, b2, g2, c2 = spot(*step)
        slot = (a1 * b_n + b1, g1 * c_n + c1)
        return pltpu.make_async_remote_copy(
            src_ref=own_ref.at[0] if own else out_ref.at[slot],
            dst_ref=out_ref.at[slot],
            send_sem=sem,
            recv_sem=recv_sem.at[slot],
            device_id=(g2 * c_n + c2, a2 * b_n + b2),
            device_id_type=MESH,
        )

    def arrived(*key):
        copy(key, (0, 0, 0, 0), own_sem, False).wait_recv()

    def sends(ka, kp, kq, own=False):
        key = (ka, kp, kq, 0)
        out = []
        if isinstance(kp, int) and kp == 0 and isinstance(kq, int) and kq == 0:
            out += [copy(key, (0, n, 0, 0), b_sem.at[ka, n], own) for n in range(1, p_n)]
        if isinstance(kq, int) and kq == 0:
            out += [copy(key, (0, 0, n, 0), g_sem.at[ka * p_n + kp, n], own) for n in range(1, q_n)]
        out += [
            copy(key, (0, 0, 0, n), c_sem.at[ka * p_n + kp, kq, n], own) for n in range(1, c_n)
        ]
        return out

    def firsts():
        return [copy((0, 0, 0, 0), (n, 0, 0, 0), a_sem.at[n], True) for n in range(1, a_n)]

    def over_a(fn):
        if a_n <= 8:
            for ka in range(1, a_n):
                fn(ka)
        elif a_n > 1:
            lax.fori_loop(1, a_n, lambda ka, _: (fn(ka), 0)[1], 0)

    def relay(ka, kp, kq):
        arrived(ka, kp, kq, 0)
        for cp in sends(ka, kp, kq):
            cp.start()

    for cp in firsts() + sends(0, 0, 0, True):
        cp.start()
    for kp in range(1, p_n):
        relay(0, kp, 0)
    for kq in range(1, q_n):
        relay(0, 0, kq)
    over_a(lambda ka: relay(ka, 0, 0))
    for kp in range(1, p_n):
        for kq in range(1, q_n):
            relay(0, kp, kq)
    over_a(lambda ka: [relay(ka, kp, 0) for kp in range(1, p_n)])
    over_a(lambda ka: [relay(ka, 0, kq) for kq in range(1, q_n)])
    over_a(lambda ka: [relay(ka, kp, kq) for kp in range(1, p_n) for kq in range(1, q_n)])

    def finish(ka):
        for kp in range(p_n):
            for kq in range(q_n):
                for kc in range(1, c_n):
                    arrived(ka, kp, kq, kc)
                for cp in sends(ka, kp, kq):
                    cp.wait_send()

    finish(0)
    over_a(finish)
    for cp in firsts():
        cp.wait_send()
    mine.wait()


def gather_latents(latents, dims):
    a_n, b_n, g_n, c_n = dims
    _, row_share, key_width = latents.shape
    n_s, n_h = a_n * b_n, g_n * c_n
    dma = pltpu.SemaphoreType.DMA
    return pl.pallas_call(
        functools.partial(gather_kernel, dims),
        out_shape=jax.ShapeDtypeStruct((n_s, n_h, row_share, key_width), latents.dtype),
        in_specs=[pl.BlockSpec(memory_space=VMEM)],
        out_specs=pl.BlockSpec(memory_space=VMEM),
        scratch_shapes=[
            dma,
            dma((a_n,)),
            dma((a_n, g_n)),
            dma((a_n * g_n, b_n)),
            dma((a_n * g_n, b_n, c_n)),
            dma((n_s, n_h)),
        ],
        compiler_params=pltpu.CompilerParams(collective_id=0, has_side_effects=True),
        name="gather_latents",
    )(latents)


def attend_kernel(scale, chunk, sel_ref, all_ref, q_ref, g_ref, o_ref, dq_ref, con_ref, keys, keys_t, acc, g_rows, o_rows):
    step = pl.program_id(0)
    block = all_ref.shape[1]
    count = sel_ref.shape[1] + 1
    tokens, heads, value_width = g_ref.shape
    f32, bf16 = jnp.float32, jnp.bfloat16

    @pl.when(step == 0)
    def _():
        for n in range(count):
            at = lax.axis_index("seq") if n == 0 else sel_ref[0, n - 1]
            rows = all_ref[at]
            keys[n * block : (n + 1) * block, :] = rows
            keys_t[:, n * block : (n + 1) * block] = rows.T
        acc[...] = jnp.zeros_like(acc)

    g_rows[...] = jnp.swapaxes(g_ref[...], 0, 1).reshape(tokens * heads, value_width)
    across = (((1,), (1,)), ((), ()))
    down = (((0,), (0,)), ((), ()))
    values = keys[:, :value_width]
    for h0 in range(0, heads, chunk):
        hs = range(h0, h0 + chunk)
        q = jnp.concatenate([q_ref[h] for h in hs], axis=1)
        g = g_rows[h0 * tokens : (h0 + chunk) * tokens, :]
        scores = jnp.dot(keys[...], q, preferred_element_type=f32)
        top = jnp.max(scores, axis=0, keepdims=True)
        weights = jnp.exp((scores - top) * scale)
        probs = weights * (1.0 / jnp.sum(weights, axis=0, keepdims=True))
        half = probs.astype(bf16)
        grad_prob = lax.dot_general(values, g, across, preferred_element_type=f32)
        delta = jnp.sum(half.astype(f32) * grad_prob, axis=0, keepdims=True)
        grad_score = (probs * (grad_prob - delta) * scale).astype(bf16)
        out = lax.dot_general(half, values, down, preferred_element_type=f32)
        dq = jnp.dot(keys_t[...], grad_score, preferred_element_type=f32).astype(bf16)
        for n, h in enumerate(hs):
            dq_ref[h] = dq[:, n * tokens : (n + 1) * tokens]
        o_rows[h0 * tokens : (h0 + chunk) * tokens, :] = out.astype(bf16)
        acc[...] += lax.dot_general(grad_score, q, across, preferred_element_type=f32)
        acc[:, :value_width] += jnp.dot(half, g, preferred_element_type=f32)
    o_ref[...] = jnp.swapaxes(o_rows[...].reshape(heads, tokens, value_width), 0, 1)

    @pl.when(step == pl.num_programs(0) - 1)
    def _():
        con_ref[...] = acc[...].astype(bf16)


def attend(selected, all_keys, queries, grad_out):
    tokens, heads, key_width = queries.shape
    value_width = grad_out.shape[2]
    keys = (selected.shape[1] + 1) * all_keys.shape[1]
    group = 8 if heads % 8 == 0 else heads
    chunk = min(4, group)
    out, dq, con = pl.pallas_call(
        functools.partial(attend_kernel, key_width ** (-0.5), chunk),
        grid=(heads // group,),
        out_shape=(
            jax.ShapeDtypeStruct((tokens, heads, value_width), jnp.bfloat16),
            jax.ShapeDtypeStruct((heads, key_width, tokens), jnp.bfloat16),
            jax.ShapeDtypeStruct((keys, key_width), jnp.bfloat16),
        ),
        in_specs=[
            pl.BlockSpec(memory_space=SMEM),
            pl.BlockSpec(all_keys.shape, lambda i: (0, 0, 0)),
            pl.BlockSpec((group, key_width, tokens), lambda i: (i, 0, 0)),
            pl.BlockSpec((tokens, group, value_width), lambda i: (0, i, 0)),
        ],
        out_specs=(
            pl.BlockSpec((tokens, group, value_width), lambda i: (0, i, 0)),
            pl.BlockSpec((group, key_width, tokens), lambda i: (i, 0, 0)),
            pl.BlockSpec((keys, key_width), lambda i: (0, 0)),
        ),
        scratch_shapes=[
            pltpu.VMEM((keys, key_width), jnp.bfloat16),
            pltpu.VMEM((key_width, keys), jnp.bfloat16),
            pltpu.VMEM((keys, key_width), jnp.float32),
            pltpu.VMEM((tokens * group, value_width), jnp.bfloat16),
            pltpu.VMEM((tokens * group, value_width), jnp.bfloat16),
        ],
        compiler_params=pltpu.CompilerParams(vmem_limit_bytes=60 * 1024 * 1024),
        name="attend",
    )(selected, all_keys, jnp.transpose(queries, (1, 2, 0)), grad_out)
    return out, jnp.transpose(dq, (2, 0, 1)), con


def reduce_kernel(
    dims, sel_ref, con_ref, out_ref,
    c_in, g_out, g_in, sums, b_out, b_in, a_out, a_in,
    c_sem, g_sem, b_sem, a_sem,
):
    a_n, b_n, g_n, c_n = dims
    me = place(dims)
    a, b, g, c = me
    count = con_ref.shape[0]
    f32, bf16 = jnp.float32, jnp.bfloat16
    greet(dims, me)

    def copy(src, dst, sems, there):
        a2, b2, g2, c2 = there
        return pltpu.make_async_remote_copy(
            src_ref=src,
            dst_ref=dst,
            send_sem=sems.at[0],
            recv_sem=sems.at[1],
            device_id=(g2 * c_n + c2, a2 * b_n + b2),
            device_id_type=MESH,
        )

    def to_c(p, k):
        c2 = other(c, k, c_n)
        return copy(con_ref.at[p, :, c2], c_in.at[p, k], c_sem.at[p, k], (a, b, g, c2))

    def to_g(p, k):
        return copy(g_out.at[p, k], g_in.at[p, k], g_sem.at[p, k], (a, b, other(g, k, g_n), c))

    def to_b(k, n):
        return copy(b_out.at[k, n], b_in.at[k, n], b_sem.at[k, n], (a, other(b, n, b_n), g, c))

    def to_a(k):
        return copy(a_out.at[k], a_in.at[k], a_sem.at[k], (other(a, k, a_n), b, g, c))

    for p in range(count):
        for k in range(1, c_n):
            to_c(p, k).start()

    def chip_sum(p, g1):
        total = con_ref[p, g1, c].astype(f32)
        for k in range(1, c_n):
            total += c_in[p, k, g1].astype(f32)
        return total

    for p in range(count):
        for k in range(1, c_n):
            to_c(p, k).wait_recv()
        for k in range(1, g_n):
            g_out[p, k] = chip_sum(p, other(g, k, g_n)).astype(bf16)
            to_g(p, k).start()
    sums[count] = jnp.zeros(sums.shape[1:], f32)
    for p in range(count):
        total = chip_sum(p, g)
        for k in range(1, g_n):
            to_g(p, k).wait_recv()
            total += g_in[p, k].astype(f32)
        sums[p] = total

    def dense(a1, b1):
        block = a1 * b_n + b1
        at = jnp.where(block == a * b_n + b, 0, count)
        for n in range(1, count):
            at = jnp.where(sel_ref[0, n - 1] == block, n, at)
        return sums[at]

    def send_b(k, _):
        for n in range(1, b_n):
            b_out[k, n] = dense(other(a, k, a_n), other(b, n, b_n)).astype(bf16)
            to_b(k, n).start()
        return 0

    def send_a(k, _):
        total = dense(other(a, k, a_n), b)
        for n in range(1, b_n):
            to_b(k, n).wait_recv()
            total += b_in[k, n].astype(f32)
        a_out[k] = total.astype(bf16)
        to_a(k).start()
        return 0

    if b_n > 1:
        lax.fori_loop(1, a_n, send_b, 0)
        send_b(0, 0)
    lax.fori_loop(1, a_n, send_a, 0)
    total = dense(a, b)
    for n in range(1, b_n):
        to_b(0, n).wait_recv()
        total += b_in[0, n].astype(f32)
    out_ref[...] = total

    def take_a(k, _):
        to_a(k).wait_recv()
        out_ref[...] += a_in[k].astype(f32)
        return 0

    lax.fori_loop(1, a_n, take_a, 0)

    def finish(k, _):
        to_a(k).wait_send()
        for n in range(1, b_n):
            to_b(k, n).wait_send()
        return 0

    lax.fori_loop(1, a_n, finish, 0)
    for n in range(1, b_n):
        to_b(0, n).wait_send()
    for p in range(count):
        for k in range(1, c_n):
            to_c(p, k).wait_send()
        for k in range(1, g_n):
            to_g(p, k).wait_send()


def reduce_grads(selected, contrib, dims):
    a_n, b_n, g_n, c_n = dims
    count = selected.shape[1] + 1
    keys, key_width = contrib.shape
    rows = keys // count // (g_n * c_n)
    contrib = contrib.reshape(count, g_n, c_n, rows, key_width)
    one = (rows, key_width)
    dma = pltpu.SemaphoreType.DMA
    half = functools.partial(pltpu.VMEM, dtype=jnp.bfloat16)
    return pl.pallas_call(
        functools.partial(reduce_kernel, dims),
        out_shape=jax.ShapeDtypeStruct(one, jnp.float32),
        in_specs=[pl.BlockSpec(memory_space=SMEM), pl.BlockSpec(memory_space=VMEM)],
        out_specs=pl.BlockSpec(memory_space=VMEM),
        scratch_shapes=[
            half((count, c_n, g_n) + one),
            half((count, g_n) + one),
            half((count, g_n) + one),
            pltpu.VMEM((count + 1,) + one, jnp.float32),
            half((a_n, b_n) + one),
            half((a_n, b_n) + one),
            half((a_n,) + one),
            half((a_n,) + one),
            dma((count, c_n, 2)),
            dma((count, g_n, 2)),
            dma((a_n, b_n, 2)),
            dma((a_n, 2)),
        ],
        compiler_params=pltpu.CompilerParams(collective_id=1, has_side_effects=True),
        name="reduce_grads",
    )(selected, contrib)


def shards(dims, queries, latents, grad_out, selected):
    assert latents.shape[0] == 1
    pieces = gather_latents(latents, dims)
    all_keys = pieces.reshape(pieces.shape[0], -1, latents.shape[2])
    output, grad_query, contrib = attend(selected, all_keys, queries, grad_out)
    return output, grad_query, reduce_grads(selected, contrib, dims)[None]


def solution(mesh):
    n_h, n_s = mesh.shape["heads"], mesh.shape["seq"]
    b_n = 2 if n_s % 2 == 0 else 1
    c_n = 2 if n_h % 2 == 0 else 1
    dims = (n_s // b_n, b_n, n_h // c_n, c_n)
    in_specs = (
        P("seq", "heads", None),
        P("seq", "heads", None),
        P("seq", "heads", None),
        P("seq", None),
    )
    out_specs = (P("seq", "heads", None), P("seq", "heads", None), P("seq", "heads", None))
    return jax.shard_map(
        functools.partial(shards, dims),
        mesh=mesh, in_specs=in_specs, out_specs=out_specs, check_vma=False,
    )
```

```python
import functools

import jax
import jax.numpy as jnp
from jax import lax
from jax.experimental import pallas as pl
from jax.experimental.pallas import tpu as pltpu
from jax.sharding import PartitionSpec as P

MESH = pl.DeviceIdType.MESH
VMEM = pltpu.MemorySpace.VMEM
SMEM = pltpu.MemorySpace.SMEM
HBM = pltpu.MemorySpace.HBM


def place(dims):
    a_n, b_n, g_n, c_n = dims
    s, h = lax.axis_index("seq"), lax.axis_index("heads")
    return s // b_n, lax.rem(s, b_n), h // c_n, lax.rem(h, c_n)


def other(x, k, n):
    return lax.rem(x + k, n)


def greet(dims, me):
    a_n, b_n, g_n, c_n = dims
    a, b, g, c = me
    barrier = pltpu.get_barrier_semaphore()

    def signal(a2, b2, g2, c2):
        pl.semaphore_signal(
            barrier, inc=1, device_id=(g2 * c_n + c2, a2 * b_n + b2), device_id_type=MESH
        )

    for k in range(1, c_n):
        signal(a, b, g, other(c, k, c_n))
    for k in range(1, b_n):
        signal(a, other(b, k, b_n), g, c)
    for k in range(1, g_n):
        signal(a, b, other(g, k, g_n), c)
    for k in range(1, a_n):
        signal(other(a, k, a_n), b, g, c)
    pl.semaphore_wait(barrier, a_n + b_n + g_n + c_n - 4)


def gather_kernel(
    dims, own_ref, g_ref, out_ref, g_out,
    g_raw, g_in_sem, own_sem, a_sem, b_sem, g_sem, c_sem, recv_sem,
):
    a_n, b_n, g_n, c_n = dims
    me = place(dims)
    a, b, g, c = me
    mine = pltpu.make_async_copy(own_ref.at[0], out_ref.at[a * b_n + b, g * c_n + c], own_sem)
    mine.start()
    staged = pltpu.make_async_copy(g_ref, g_raw, g_in_sem)
    staged.start()
    greet(dims, me)

    swap = b_n == g_n
    flip = lax.rem(c, 2) if swap else 0

    def spot(ka, kp, kq, kc):
        kb, kg = (flip * kp + (1 - flip) * kq, (1 - flip) * kp + flip * kq) if swap else (kq, kp)
        return other(a, ka, a_n), other(b, kb, b_n), other(g, kg, g_n), other(c, kc, c_n)

    p_n, q_n = g_n, b_n

    def copy(key, step, sem, own):
        a1, b1, g1, c1 = spot(*key)
        a2, b2, g2, c2 = spot(*step)
        slot = (a1 * b_n + b1, g1 * c_n + c1)
        return pltpu.make_async_remote_copy(
            src_ref=own_ref.at[0] if own else out_ref.at[slot],
            dst_ref=out_ref.at[slot],
            send_sem=sem,
            recv_sem=recv_sem.at[slot],
            device_id=(g2 * c_n + c2, a2 * b_n + b2),
            device_id_type=MESH,
        )

    def arrived(*key):
        copy(key, (0, 0, 0, 0), own_sem, False).wait_recv()

    def sends(ka, kp, kq, own=False):
        key = (ka, kp, kq, 0)
        out = []
        if isinstance(kp, int) and kp == 0 and isinstance(kq, int) and kq == 0:
            out += [copy(key, (0, n, 0, 0), b_sem.at[ka, n], own) for n in range(1, p_n)]
        if isinstance(kq, int) and kq == 0:
            out += [copy(key, (0, 0, n, 0), g_sem.at[ka * p_n + kp, n], own) for n in range(1, q_n)]
        out += [
            copy(key, (0, 0, 0, n), c_sem.at[ka * p_n + kp, kq, n], own) for n in range(1, c_n)
        ]
        return out

    def firsts():
        return [copy((0, 0, 0, 0), (n, 0, 0, 0), a_sem.at[n], True) for n in range(1, a_n)]

    def over_a(fn):
        if a_n <= 8:
            for ka in range(1, a_n):
                fn(ka)
        elif a_n > 1:
            lax.fori_loop(1, a_n, lambda ka, _: (fn(ka), 0)[1], 0)

    def relay(ka, kp, kq):
        arrived(ka, kp, kq, 0)
        for cp in sends(ka, kp, kq):
            cp.start()

    for cp in firsts() + sends(0, 0, 0, True):
        cp.start()
    staged.wait()
    g_out[...] = jnp.swapaxes(g_raw[...], 0, 1)
    for kp in range(1, p_n):
        relay(0, kp, 0)
    for kq in range(1, q_n):
        relay(0, 0, kq)
    over_a(lambda ka: relay(ka, 0, 0))
    for kp in range(1, p_n):
        for kq in range(1, q_n):
            relay(0, kp, kq)
    over_a(lambda ka: [relay(ka, kp, 0) for kp in range(1, p_n)])
    over_a(lambda ka: [relay(ka, 0, kq) for kq in range(1, q_n)])
    over_a(lambda ka: [relay(ka, kp, kq) for kp in range(1, p_n) for kq in range(1, q_n)])

    def finish(ka):
        for kp in range(p_n):
            for kq in range(q_n):
                for kc in range(1, c_n):
                    arrived(ka, kp, kq, kc)
                for cp in sends(ka, kp, kq):
                    cp.wait_send()

    finish(0)
    over_a(finish)
    for cp in firsts():
        cp.wait_send()
    mine.wait()


def gather_latents(latents, grad_out, dims):
    a_n, b_n, g_n, c_n = dims
    _, row_share, key_width = latents.shape
    n_s, n_h = a_n * b_n, g_n * c_n
    tokens, heads, value_width = grad_out.shape
    dma = pltpu.SemaphoreType.DMA
    return pl.pallas_call(
        functools.partial(gather_kernel, dims),
        out_shape=(
            jax.ShapeDtypeStruct((n_s, n_h, row_share, key_width), latents.dtype),
            jax.ShapeDtypeStruct((heads, tokens, value_width), grad_out.dtype),
        ),
        in_specs=[pl.BlockSpec(memory_space=HBM)] * 2,
        out_specs=[pl.BlockSpec(memory_space=VMEM)] * 2,
        scratch_shapes=[
            pltpu.VMEM(grad_out.shape, grad_out.dtype),
            dma,
            dma,
            dma((a_n,)),
            dma((a_n, g_n)),
            dma((a_n * g_n, b_n)),
            dma((a_n * g_n, b_n, c_n)),
            dma((n_s, n_h)),
        ],
        compiler_params=pltpu.CompilerParams(collective_id=0, has_side_effects=True, vmem_limit_bytes=67043328 - 14000000),
        name="gather_latents",
    )(latents, grad_out)


def attend_kernel(scale, chunk, sel_ref, all_ref, q_ref, g_ref, o_ref, dq_ref, con_ref, keys, keys_t, acc, o_rows):
    step = pl.program_id(0)
    block = all_ref.shape[1]
    count = sel_ref.shape[1] + 1
    heads, tokens, value_width = g_ref.shape
    f32, bf16 = jnp.float32, jnp.bfloat16

    @pl.when(step == 0)
    def _():
        for n in range(count):
            at = lax.axis_index("seq") if n == 0 else sel_ref[0, n - 1]
            rows = all_ref[at]
            keys[n * block : (n + 1) * block, :] = rows
            keys_t[:, n * block : (n + 1) * block] = rows.T
        acc[...] = jnp.zeros_like(acc)

    across = (((1,), (1,)), ((), ()))
    down = (((0,), (0,)), ((), ()))
    values = keys[:, :value_width]
    for h0 in range(0, heads, chunk):
        hs = range(h0, h0 + chunk)
        q = jnp.concatenate([q_ref[h] for h in hs], axis=1)
        g = g_ref[h0 : h0 + chunk].reshape(chunk * tokens, value_width)
        scores = jnp.dot(keys[...], q, preferred_element_type=f32)
        top = jnp.max(scores, axis=0, keepdims=True)
        weights = jnp.exp((scores - top) * scale)
        probs = weights * (1.0 / jnp.sum(weights, axis=0, keepdims=True))
        half = probs.astype(bf16)
        grad_prob = lax.dot_general(values, g, across, preferred_element_type=f32)
        delta = jnp.sum(half.astype(f32) * grad_prob, axis=0, keepdims=True)
        grad_score = (probs * (grad_prob - delta) * scale).astype(bf16)
        out = lax.dot_general(half, values, down, preferred_element_type=f32)
        dq = jnp.dot(keys_t[...], grad_score, preferred_element_type=f32).astype(bf16)
        for n, h in enumerate(hs):
            dq_ref[h] = dq[:, n * tokens : (n + 1) * tokens]
        o_rows[h0 * tokens : (h0 + chunk) * tokens, :] = out.astype(bf16)
        acc[...] += lax.dot_general(grad_score, q, across, preferred_element_type=f32)
        acc[:, :value_width] += jnp.dot(half, g, preferred_element_type=f32)
    o_ref[...] = jnp.swapaxes(o_rows[...].reshape(heads, tokens, value_width), 0, 1)

    @pl.when(step == pl.num_programs(0) - 1)
    def _():
        con_ref[...] = acc[...].astype(bf16)


def attend(selected, all_keys, queries, grad_out):
    heads, key_width, tokens = queries.shape
    value_width = grad_out.shape[2]
    keys = (selected.shape[1] + 1) * all_keys.shape[1]
    group = 8 if heads % 8 == 0 else heads
    chunk = min(4, group)
    out, dq, con = pl.pallas_call(
        functools.partial(attend_kernel, key_width ** (-0.5), chunk),
        grid=(heads // group,),
        out_shape=(
            jax.ShapeDtypeStruct((tokens, heads, value_width), jnp.bfloat16),
            jax.ShapeDtypeStruct((heads, key_width, tokens), jnp.bfloat16),
            jax.ShapeDtypeStruct((keys, key_width), jnp.bfloat16),
        ),
        in_specs=[
            pl.BlockSpec(memory_space=SMEM),
            pl.BlockSpec(all_keys.shape, lambda i: (0, 0, 0)),
            pl.BlockSpec((group, key_width, tokens), lambda i: (i, 0, 0)),
            pl.BlockSpec((group, tokens, value_width), lambda i: (i, 0, 0)),
        ],
        out_specs=(
            pl.BlockSpec((tokens, group, value_width), lambda i: (0, i, 0)),
            pl.BlockSpec((group, key_width, tokens), lambda i: (i, 0, 0)),
            pl.BlockSpec((keys, key_width), lambda i: (0, 0)),
        ),
        scratch_shapes=[
            pltpu.VMEM((keys, key_width), jnp.bfloat16),
            pltpu.VMEM((key_width, keys), jnp.bfloat16),
            pltpu.VMEM((keys, key_width), jnp.float32),
            pltpu.VMEM((tokens * group, value_width), jnp.bfloat16),
        ],
        compiler_params=pltpu.CompilerParams(vmem_limit_bytes=67043328 - 16000000),
        name="attend",
    )(selected, all_keys, queries, grad_out)
    return out, jnp.transpose(dq, (2, 0, 1)), con


def reduce_kernel(
    dims, sel_ref, con_ref, out_ref,
    c_in, g_out, g_in, sums, b_out, b_in, a_out, a_in,
    c_sem, g_sem, b_sem, a_sem,
):
    a_n, b_n, g_n, c_n = dims
    me = place(dims)
    a, b, g, c = me
    count = con_ref.shape[0]
    f32, bf16 = jnp.float32, jnp.bfloat16
    greet(dims, me)

    def copy(src, dst, sems, there):
        a2, b2, g2, c2 = there
        return pltpu.make_async_remote_copy(
            src_ref=src,
            dst_ref=dst,
            send_sem=sems.at[0],
            recv_sem=sems.at[1],
            device_id=(g2 * c_n + c2, a2 * b_n + b2),
            device_id_type=MESH,
        )

    def to_c(p, k):
        c2 = other(c, k, c_n)
        return copy(con_ref.at[p, :, c2], c_in.at[p, k], c_sem.at[p, k], (a, b, g, c2))

    def to_g(p, k):
        return copy(g_out.at[p, k], g_in.at[p, k], g_sem.at[p, k], (a, b, other(g, k, g_n), c))

    def to_b(k, n):
        return copy(b_out.at[k, n], b_in.at[k, n], b_sem.at[k, n], (a, other(b, n, b_n), g, c))

    def to_a(k):
        return copy(a_out.at[k], a_in.at[k], a_sem.at[k], (other(a, k, a_n), b, g, c))

    order = list(range(1, count)) + [0]
    for p in order:
        for k in range(1, c_n):
            to_c(p, k).start()

    def chip_sum(p, g1):
        total = con_ref[p, g1, c].astype(f32)
        for k in range(1, c_n):
            total += c_in[p, k, g1].astype(f32)
        return total

    for p in order:
        for k in range(1, c_n):
            to_c(p, k).wait_recv()
        for k in range(1, g_n):
            g_out[p, k] = chip_sum(p, other(g, k, g_n)).astype(bf16)
            to_g(p, k).start()

    def head_sum(p):
        total = chip_sum(p, g)
        for k in range(1, g_n):
            to_g(p, k).wait_recv()
            total += g_in[p, k].astype(f32)
        return total

    sums[0] = jnp.zeros(sums.shape[1:], f32)
    for p in range(1, count):
        sums[p] = head_sum(p)

    def dense(a1, b1):
        block = a1 * b_n + b1
        at = 0
        for n in range(1, count):
            at = jnp.where(sel_ref[0, n - 1] == block, n, at)
        return sums[at]

    def send_b(k, _):
        for n in range(1, b_n):
            b_out[k, n] = dense(other(a, k, a_n), other(b, n, b_n)).astype(bf16)
            to_b(k, n).start()
        return 0

    def send_a(k, _):
        total = dense(other(a, k, a_n), b)
        for n in range(1, b_n):
            to_b(k, n).wait_recv()
            total += b_in[k, n].astype(f32)
        a_out[k] = total.astype(bf16)
        to_a(k).start()
        return 0

    if b_n > 1:
        lax.fori_loop(1, a_n, send_b, 0)
        send_b(0, 0)
    lax.fori_loop(1, a_n, send_a, 0)
    total = head_sum(0)
    for n in range(1, b_n):
        to_b(0, n).wait_recv()
        total += b_in[0, n].astype(f32)
    out_ref[...] = total

    def take_a(k, _):
        to_a(k).wait_recv()
        out_ref[...] += a_in[k].astype(f32)
        return 0

    lax.fori_loop(1, a_n, take_a, 0)

    def finish(k, _):
        to_a(k).wait_send()
        for n in range(1, b_n):
            to_b(k, n).wait_send()
        return 0

    lax.fori_loop(1, a_n, finish, 0)
    for n in range(1, b_n):
        to_b(0, n).wait_send()
    for p in range(count):
        for k in range(1, c_n):
            to_c(p, k).wait_send()
        for k in range(1, g_n):
            to_g(p, k).wait_send()


def reduce_grads(selected, contrib, dims):
    a_n, b_n, g_n, c_n = dims
    count = selected.shape[1] + 1
    keys, key_width = contrib.shape
    rows = keys // count // (g_n * c_n)
    contrib = contrib.reshape(count, g_n, c_n, rows, key_width)
    one = (rows, key_width)
    dma = pltpu.SemaphoreType.DMA
    half = functools.partial(pltpu.VMEM, dtype=jnp.bfloat16)
    return pl.pallas_call(
        functools.partial(reduce_kernel, dims),
        out_shape=jax.ShapeDtypeStruct(one, jnp.float32),
        in_specs=[pl.BlockSpec(memory_space=SMEM), pl.BlockSpec(memory_space=VMEM)],
        out_specs=pl.BlockSpec(memory_space=VMEM),
        scratch_shapes=[
            half((count, c_n, g_n) + one),
            half((count, g_n) + one),
            half((count, g_n) + one),
            pltpu.VMEM((count,) + one, jnp.float32),
            half((a_n, b_n) + one),
            half((a_n, b_n) + one),
            half((a_n,) + one),
            half((a_n,) + one),
            dma((count, c_n, 2)),
            dma((count, g_n, 2)),
            dma((a_n, b_n, 2)),
            dma((a_n, 2)),
        ],
        compiler_params=pltpu.CompilerParams(collective_id=1, has_side_effects=True, vmem_limit_bytes=12 * 1024 * 1024),
        name="reduce_grads",
    )(selected, contrib)


def shards(dims, queries, latents, grad_out, selected):
    assert latents.shape[0] == 1
    pieces, grad_out = gather_latents(latents, grad_out, dims)
    all_keys = pieces.reshape(pieces.shape[0], -1, latents.shape[2])
    output, grad_query, contrib = attend(
        selected, all_keys, jnp.transpose(queries, (1, 2, 0)), grad_out
    )
    return output, grad_query, reduce_grads(selected, contrib, dims)[None]


def solution(mesh):
    n_h, n_s = mesh.shape["heads"], mesh.shape["seq"]
    b_n = 2 if n_s % 2 == 0 else 1
    c_n = 2 if n_h % 2 == 0 else 1
    dims = (n_s // b_n, b_n, n_h // c_n, c_n)
    in_specs = (
        P("seq", "heads", None),
        P("seq", "heads", None),
        P("seq", "heads", None),
        P("seq", None),
    )
    out_specs = (P("seq", "heads", None), P("seq", "heads", None), P("seq", "heads", None))
    return jax.shard_map(
        functools.partial(shards, dims),
        mesh=mesh, in_specs=in_specs, out_specs=out_specs, check_vma=False,
    )
```

```python
import functools

import jax
import jax.numpy as jnp
from jax import lax
from jax.experimental import pallas as pl
from jax.experimental.pallas import tpu as pltpu
from jax.sharding import PartitionSpec as P

MESH = pl.DeviceIdType.MESH
VMEM = pltpu.MemorySpace.VMEM
SMEM = pltpu.MemorySpace.SMEM
HBM = pltpu.MemorySpace.HBM


def place(dims):
    a_n, b_n, g_n, c_n = dims
    s, h = lax.axis_index("seq"), lax.axis_index("heads")
    return s // b_n, lax.rem(s, b_n), h // c_n, lax.rem(h, c_n)


def other(x, k, n):
    return lax.rem(x + k, n)


def greet(dims, me):
    a_n, b_n, g_n, c_n = dims
    a, b, g, c = me
    barrier = pltpu.get_barrier_semaphore()

    def signal(a2, b2, g2, c2):
        pl.semaphore_signal(
            barrier, inc=1, device_id=(g2 * c_n + c2, a2 * b_n + b2), device_id_type=MESH
        )

    for k in range(1, c_n):
        signal(a, b, g, other(c, k, c_n))
    for k in range(1, b_n):
        signal(a, other(b, k, b_n), g, c)
    for k in range(1, g_n):
        signal(a, b, other(g, k, g_n), c)
    for k in range(1, a_n):
        signal(other(a, k, a_n), b, g, c)
    pl.semaphore_wait(barrier, a_n + b_n + g_n + c_n - 4)


def gather_kernel(
    dims, own_ref, g_ref, out_ref, g_out,
    g_raw, g_in_sem, own_sem, a_sem, b_sem, g_sem, c_sem, recv_sem,
):
    a_n, b_n, g_n, c_n = dims
    me = place(dims)
    a, b, g, c = me
    mine = pltpu.make_async_copy(own_ref.at[0], out_ref.at[a * b_n + b, g * c_n + c], own_sem)
    mine.start()
    staged = pltpu.make_async_copy(g_ref, g_raw, g_in_sem)
    staged.start()
    greet(dims, me)

    swap = b_n == g_n
    flip = lax.rem(c, 2) if swap else 0

    def spot(ka, kp, kq, kc):
        kb, kg = (flip * kp + (1 - flip) * kq, (1 - flip) * kp + flip * kq) if swap else (kq, kp)
        return other(a, ka, a_n), other(b, kb, b_n), other(g, kg, g_n), other(c, kc, c_n)

    p_n, q_n = g_n, b_n

    def copy(key, step, sem, own):
        a1, b1, g1, c1 = spot(*key)
        a2, b2, g2, c2 = spot(*step)
        slot = (a1 * b_n + b1, g1 * c_n + c1)
        return pltpu.make_async_remote_copy(
            src_ref=own_ref.at[0] if own else out_ref.at[slot],
            dst_ref=out_ref.at[slot],
            send_sem=sem,
            recv_sem=recv_sem.at[slot],
            device_id=(g2 * c_n + c2, a2 * b_n + b2),
            device_id_type=MESH,
        )

    def arrived(*key):
        copy(key, (0, 0, 0, 0), own_sem, False).wait_recv()

    def sends(ka, kp, kq, own=False):
        key = (ka, kp, kq, 0)
        out = []
        if isinstance(kp, int) and kp == 0 and isinstance(kq, int) and kq == 0:
            out += [copy(key, (0, n, 0, 0), b_sem.at[ka, n], own) for n in range(1, p_n)]
        if isinstance(kq, int) and kq == 0:
            out += [copy(key, (0, 0, n, 0), g_sem.at[ka * p_n + kp, n], own) for n in range(1, q_n)]
        out += [
            copy(key, (0, 0, 0, n), c_sem.at[ka * p_n + kp, kq, n], own) for n in range(1, c_n)
        ]
        return out

    def firsts():
        return [copy((0, 0, 0, 0), (n, 0, 0, 0), a_sem.at[n], True) for n in range(1, a_n)]

    def over_a(fn):
        if a_n <= 8:
            for ka in range(1, a_n):
                fn(ka)
        elif a_n > 1:
            lax.fori_loop(1, a_n, lambda ka, _: (fn(ka), 0)[1], 0)

    def relay(ka, kp, kq):
        arrived(ka, kp, kq, 0)
        for cp in sends(ka, kp, kq):
            cp.start()

    for cp in firsts() + sends(0, 0, 0, True):
        cp.start()
    staged.wait()
    g_out[...] = jnp.swapaxes(g_raw[...], 0, 1)
    for kp in range(1, p_n):
        relay(0, kp, 0)
    for kq in range(1, q_n):
        relay(0, 0, kq)
    over_a(lambda ka: relay(ka, 0, 0))
    for kp in range(1, p_n):
        for kq in range(1, q_n):
            relay(0, kp, kq)
    over_a(lambda ka: [relay(ka, kp, 0) for kp in range(1, p_n)])
    over_a(lambda ka: [relay(ka, 0, kq) for kq in range(1, q_n)])
    over_a(lambda ka: [relay(ka, kp, kq) for kp in range(1, p_n) for kq in range(1, q_n)])

    def finish(ka):
        for kp in range(p_n):
            for kq in range(q_n):
                for kc in range(1, c_n):
                    arrived(ka, kp, kq, kc)
                for cp in sends(ka, kp, kq):
                    cp.wait_send()

    finish(0)
    over_a(finish)
    for cp in firsts():
        cp.wait_send()
    mine.wait()


def gather_latents(latents, grad_out, dims):
    a_n, b_n, g_n, c_n = dims
    _, row_share, key_width = latents.shape
    n_s, n_h = a_n * b_n, g_n * c_n
    tokens, heads, value_width = grad_out.shape
    dma = pltpu.SemaphoreType.DMA
    return pl.pallas_call(
        functools.partial(gather_kernel, dims),
        out_shape=(
            jax.ShapeDtypeStruct((n_s, n_h, row_share, key_width), latents.dtype),
            jax.ShapeDtypeStruct((heads, tokens, value_width), grad_out.dtype),
        ),
        in_specs=[pl.BlockSpec(memory_space=HBM)] * 2,
        out_specs=[pl.BlockSpec(memory_space=VMEM)] * 2,
        scratch_shapes=[
            pltpu.VMEM(grad_out.shape, grad_out.dtype),
            dma,
            dma,
            dma((a_n,)),
            dma((a_n, g_n)),
            dma((a_n * g_n, b_n)),
            dma((a_n * g_n, b_n, c_n)),
            dma((n_s, n_h)),
        ],
        compiler_params=pltpu.CompilerParams(collective_id=0, has_side_effects=True, vmem_limit_bytes=67043328 - 14000000),
        name="gather_latents",
    )(latents, grad_out)


def attend_kernel(scale, chunk, sel_ref, all_ref, q_ref, g_ref, o_ref, dq_ref, con_ref, keys, keys_t, acc, o_rows):
    step = pl.program_id(0)
    block = all_ref.shape[1]
    count = sel_ref.shape[1] + 1
    heads, tokens, value_width = g_ref.shape
    f32, bf16 = jnp.float32, jnp.bfloat16

    @pl.when(step == 0)
    def _():
        for n in range(count):
            at = lax.axis_index("seq") if n == 0 else sel_ref[0, n - 1]
            rows = all_ref[at]
            keys[n * block : (n + 1) * block, :] = rows
            keys_t[:, n * block : (n + 1) * block] = rows.T
        acc[...] = jnp.zeros_like(acc)

    across = (((1,), (1,)), ((), ()))
    down = (((0,), (0,)), ((), ()))
    values = keys[:, :value_width]
    for h0 in range(0, heads, chunk):
        hs = range(h0, h0 + chunk)
        q = jnp.concatenate([q_ref[h] for h in hs], axis=1)
        g = g_ref[h0 : h0 + chunk].reshape(chunk * tokens, value_width)
        scores = jnp.dot(keys[...], q, preferred_element_type=f32)
        top = jnp.max(scores, axis=0, keepdims=True)
        weights = jnp.exp((scores - top) * scale)
        probs = weights * (1.0 / jnp.sum(weights, axis=0, keepdims=True))
        half = probs.astype(bf16)
        grad_prob = lax.dot_general(values, g, across, preferred_element_type=f32)
        delta = jnp.sum(half.astype(f32) * grad_prob, axis=0, keepdims=True)
        grad_score = (probs * (grad_prob - delta) * scale).astype(bf16)
        out = lax.dot_general(half, values, down, preferred_element_type=f32)
        dq = jnp.dot(keys_t[...], grad_score, preferred_element_type=f32).astype(bf16)
        for n, h in enumerate(hs):
            dq_ref[h] = dq[:, n * tokens : (n + 1) * tokens]
        o_rows[h0 * tokens : (h0 + chunk) * tokens, :] = out.astype(bf16)
        acc[...] += lax.dot_general(grad_score, q, across, preferred_element_type=f32)
        acc[:, :value_width] += jnp.dot(half, g, preferred_element_type=f32)
    o_ref[...] = jnp.swapaxes(o_rows[...].reshape(heads, tokens, value_width), 0, 1)

    @pl.when(step == pl.num_programs(0) - 1)
    def _():
        con_ref[...] = acc[...].astype(bf16)


def attend(selected, all_keys, queries, grad_out):
    heads, key_width, tokens = queries.shape
    value_width = grad_out.shape[2]
    keys = (selected.shape[1] + 1) * all_keys.shape[1]
    group = 8 if heads % 8 == 0 else heads
    chunk = min(8, group)
    out, dq, con = pl.pallas_call(
        functools.partial(attend_kernel, key_width ** (-0.5), chunk),
        grid=(heads // group,),
        out_shape=(
            jax.ShapeDtypeStruct((tokens, heads, value_width), jnp.bfloat16),
            jax.ShapeDtypeStruct((heads, key_width, tokens), jnp.bfloat16),
            jax.ShapeDtypeStruct((keys, key_width), jnp.bfloat16),
        ),
        in_specs=[
            pl.BlockSpec(memory_space=SMEM),
            pl.BlockSpec(all_keys.shape, lambda i: (0, 0, 0)),
            pl.BlockSpec((group, key_width, tokens), lambda i: (i, 0, 0)),
            pl.BlockSpec((group, tokens, value_width), lambda i: (i, 0, 0)),
        ],
        out_specs=(
            pl.BlockSpec((tokens, group, value_width), lambda i: (0, i, 0)),
            pl.BlockSpec((group, key_width, tokens), lambda i: (i, 0, 0)),
            pl.BlockSpec((keys, key_width), lambda i: (0, 0)),
        ),
        scratch_shapes=[
            pltpu.VMEM((keys, key_width), jnp.bfloat16),
            pltpu.VMEM((key_width, keys), jnp.bfloat16),
            pltpu.VMEM((keys, key_width), jnp.float32),
            pltpu.VMEM((tokens * group, value_width), jnp.bfloat16),
        ],
        compiler_params=pltpu.CompilerParams(vmem_limit_bytes=67043328 - 16000000),
        name="attend",
    )(selected, all_keys, queries, grad_out)
    return out, jnp.transpose(dq, (2, 0, 1)), con


def reduce_kernel(
    dims, sel_ref, con_ref, out_ref,
    c_in, g_out, g_in, sums, b_out, b_in, a_out, a_in,
    c_sem, g_sem, b_sem, a_sem,
):
    a_n, b_n, g_n, c_n = dims
    me = place(dims)
    a, b, g, c = me
    count = con_ref.shape[0]
    f32, bf16 = jnp.float32, jnp.bfloat16
    greet(dims, me)

    def copy(src, dst, sems, there):
        a2, b2, g2, c2 = there
        return pltpu.make_async_remote_copy(
            src_ref=src,
            dst_ref=dst,
            send_sem=sems.at[0],
            recv_sem=sems.at[1],
            device_id=(g2 * c_n + c2, a2 * b_n + b2),
            device_id_type=MESH,
        )

    def to_c(p, k):
        c2 = other(c, k, c_n)
        return copy(con_ref.at[p, :, c2], c_in.at[p, k], c_sem.at[p, k], (a, b, g, c2))

    def to_g(p, k):
        return copy(g_out.at[p, k], g_in.at[p, k], g_sem.at[p, k], (a, b, other(g, k, g_n), c))

    def to_b(k, n):
        return copy(b_out.at[k, n], b_in.at[k, n], b_sem.at[k, n], (a, other(b, n, b_n), g, c))

    def to_a(k):
        return copy(a_out.at[k], a_in.at[k], a_sem.at[k], (other(a, k, a_n), b, g, c))

    order = list(range(1, count)) + [0]
    for p in order:
        for k in range(1, c_n):
            to_c(p, k).start()

    def chip_sum(p, g1):
        total = con_ref[p, g1, c].astype(f32)
        for k in range(1, c_n):
            total += c_in[p, k, g1].astype(f32)
        return total

    for p in order:
        for k in range(1, c_n):
            to_c(p, k).wait_recv()
        for k in range(1, g_n):
            g_out[p, k] = chip_sum(p, other(g, k, g_n)).astype(bf16)
            to_g(p, k).start()

    def head_sum(p):
        total = chip_sum(p, g)
        for k in range(1, g_n):
            to_g(p, k).wait_recv()
            total += g_in[p, k].astype(f32)
        return total

    sums[0] = jnp.zeros(sums.shape[1:], f32)
    for p in range(1, count):
        sums[p] = head_sum(p)

    def dense(a1, b1):
        block = a1 * b_n + b1
        at = 0
        for n in range(1, count):
            at = jnp.where(sel_ref[0, n - 1] == block, n, at)
        return sums[at]

    def send_b(k, _):
        for n in range(1, b_n):
            b_out[k, n] = dense(other(a, k, a_n), other(b, n, b_n)).astype(bf16)
            to_b(k, n).start()
        return 0

    def send_a(k, _):
        total = dense(other(a, k, a_n), b)
        for n in range(1, b_n):
            to_b(k, n).wait_recv()
            total += b_in[k, n].astype(f32)
        a_out[k] = total.astype(bf16)
        to_a(k).start()
        return 0

    if b_n > 1:
        lax.fori_loop(1, a_n, send_b, 0)
        send_b(0, 0)
    lax.fori_loop(1, a_n, send_a, 0)
    total = head_sum(0)
    for n in range(1, b_n):
        to_b(0, n).wait_recv()
        total += b_in[0, n].astype(f32)
    out_ref[...] = total

    def take_a(k, _):
        to_a(k).wait_recv()
        out_ref[...] += a_in[k].astype(f32)
        return 0

    lax.fori_loop(1, a_n, take_a, 0)

    def finish(k, _):
        to_a(k).wait_send()
        for n in range(1, b_n):
            to_b(k, n).wait_send()
        return 0

    lax.fori_loop(1, a_n, finish, 0)
    for n in range(1, b_n):
        to_b(0, n).wait_send()
    for p in range(count):
        for k in range(1, c_n):
            to_c(p, k).wait_send()
        for k in range(1, g_n):
            to_g(p, k).wait_send()


def reduce_grads(selected, contrib, dims):
    a_n, b_n, g_n, c_n = dims
    count = selected.shape[1] + 1
    keys, key_width = contrib.shape
    rows = keys // count // (g_n * c_n)
    contrib = contrib.reshape(count, g_n, c_n, rows, key_width)
    one = (rows, key_width)
    dma = pltpu.SemaphoreType.DMA
    half = functools.partial(pltpu.VMEM, dtype=jnp.bfloat16)
    return pl.pallas_call(
        functools.partial(reduce_kernel, dims),
        out_shape=jax.ShapeDtypeStruct(one, jnp.float32),
        in_specs=[pl.BlockSpec(memory_space=SMEM), pl.BlockSpec(memory_space=VMEM)],
        out_specs=pl.BlockSpec(memory_space=VMEM),
        scratch_shapes=[
            half((count, c_n, g_n) + one),
            half((count, g_n) + one),
            half((count, g_n) + one),
            pltpu.VMEM((count,) + one, jnp.float32),
            half((a_n, b_n) + one),
            half((a_n, b_n) + one),
            half((a_n,) + one),
            half((a_n,) + one),
            dma((count, c_n, 2)),
            dma((count, g_n, 2)),
            dma((a_n, b_n, 2)),
            dma((a_n, 2)),
        ],
        compiler_params=pltpu.CompilerParams(collective_id=1, has_side_effects=True, vmem_limit_bytes=12 * 1024 * 1024),
        name="reduce_grads",
    )(selected, contrib)


def shards(dims, queries, latents, grad_out, selected):
    assert latents.shape[0] == 1
    pieces, grad_out = gather_latents(latents, grad_out, dims)
    all_keys = pieces.reshape(pieces.shape[0], -1, latents.shape[2])
    output, grad_query, contrib = attend(
        selected, all_keys, jnp.transpose(queries, (1, 2, 0)), grad_out
    )
    return output, grad_query, reduce_grads(selected, contrib, dims)[None]


def solution(mesh):
    n_h, n_s = mesh.shape["heads"], mesh.shape["seq"]
    b_n = 2 if n_s % 2 == 0 else 1
    c_n = 2 if n_h % 2 == 0 else 1
    dims = (n_s // b_n, b_n, n_h // c_n, c_n)
    in_specs = (
        P("seq", "heads", None),
        P("seq", "heads", None),
        P("seq", "heads", None),
        P("seq", None),
    )
    out_specs = (P("seq", "heads", None), P("seq", "heads", None), P("seq", "heads", None))
    return jax.shard_map(
        functools.partial(shards, dims),
        mesh=mesh, in_specs=in_specs, out_specs=out_specs, check_vma=False,
    )
```
